128 devices in a mesh: seq: 32 (over y, x, z_lo), dp: 4 (over z_hi, core).
Axes of the slice: x: 4, y: 4, z: 4 (z_hi: 2, z_lo: 2; z = z_hi * 2 + z_lo), core: 2. Of those that a mesh axis runs over, the one named last changes fastest.
Arguments:
- queries: bfloat16 [4, 32, 1024, 1024], P('dp', 'seq'), may hold values from -6 to 6
- keys: bfloat16 [4, 32, 1024, 1024], P('dp', 'seq'), may hold values from -6 to 6
- values: bfloat16 [4, 32, 1024, 1024], P('dp', 'seq'), may hold values from -6 to 6
- out_weight: bfloat16 [1024, 2048], P(('seq', 'dp')), may hold values from -0.1875 to 0.1875
- cotangent: bfloat16 [4, 32, 1024, 2048], P('dp', 'seq'), may hold values from -6 to 6
Outputs:
- layer_out: bfloat16 [4, 32, 1024, 2048], P('dp', 'seq')
- query_grad: bfloat16 [4, 32, 1024, 1024], P('dp', 'seq')
- key_grad: bfloat16 [4, 32, 1024, 1024], P('dp', 'seq')
- value_grad: bfloat16 [4, 32, 1024, 1024], P('dp', 'seq')
- weight_grad: float32 [1024, 2048], P(('seq', 'dp'))
The draws below stay inside these ranges and needn't reach their ends.
All inputs are finite; a program needn't handle non-finite values.
Results may differ from the reference program's by a relative error of at most 0.0071.
Values may be sent and summed in bfloat16 or wider, within the bound.
A program may use at most 128 MiB of HBM per device.

```python
import math
import jax
import jax.numpy as jnp
from jax import lax

D = 2048
ROW_HEADS = 4
COL_HEADS = 4
DH = 128
STRIDE = 1024
ROWS = 32
SEQS = 4
ALL_TOKENS = 131072


def drawn_draw(key, salt):
    head_width = (ROW_HEADS + COL_HEADS) * DH
    noise = jax.random.truncated_normal(jax.random.fold_in(key, salt), -4.0, 4.0, (SEQS, ROWS, STRIDE, head_width), jnp.float32) * 1.4
    return noise


def draw_queries(key, part):
    return drawn_draw(key, 11).astype(jnp.bfloat16)


def draw_keys(key, part):
    return drawn_draw(key, 13).astype(jnp.bfloat16)


def level_of(own_key, extent, pieces, smallest, largest):
    factor_of = 1.0
    for position, blocks in pieces:
        steps = jax.random.uniform(jax.random.fold_in(jax.random.fold_in(own_key, 6), position), (blocks,), jnp.float32, smallest / len(pieces), largest / len(pieces))
        factor_of = factor_of * jnp.repeat(jnp.exp(steps), extent[position] // blocks).reshape((-1,) + (1,) * (len(extent) - 1 - position))
    return factor_of


def centred(own_key, dims, scale, most, cuts=(), dtype=jnp.bfloat16):
    result = jax.random.normal(own_key, dims, jnp.float32) * scale
    if len(cuts) > 0:
        result = level_of(own_key, dims, cuts, -0.22, 0.18) * result
    return jnp.clip(result, min=-most, max=most).astype(dtype)


def setup_inputs(seed: int = 0) -> dict:
    streams_of = jax.random.split(jax.random.key(seed), 6)
    queries = draw_queries(jax.random.fold_in(streams_of[5], 71), 0)
    keys = draw_keys(jax.random.fold_in(streams_of[5], 71), 0)
    values = centred(streams_of[2], (SEQS, ROWS, STRIDE, (ROW_HEADS + COL_HEADS) * DH), 1.0, 6.0, ((0, 4), (1, 32)))
    out_weight = centred(streams_of[3], ((ROW_HEADS + COL_HEADS) * DH, D), ((ROW_HEADS + COL_HEADS) * DH) ** -0.5, 0.1875, ((0, 128),))
    cotangent = centred(streams_of[4], (SEQS, ROWS, STRIDE, D), 1.0, 6.0, ((0, 4), (1, 32)))
    return dict(queries=queries, keys=keys, values=values, out_weight=out_weight, cotangent=cotangent)


def attend_sets(query_set, key_set, value_set, upstream_set):
    factor = 1.0 / math.sqrt(query_set.shape[-1])
    query_wide = query_set.astype(jnp.float32)
    key_wide = key_set.astype(jnp.float32)
    value_wide = value_set.astype(jnp.float32)
    upstream_wide = upstream_set.astype(jnp.float32)
    scores = jnp.einsum('...ld,...md->...lm', query_wide, key_wide) * factor
    length = scores.shape[-1]
    masked_out = lax.broadcasted_iota(jnp.int32, (length, length), 1) > lax.broadcasted_iota(jnp.int32, (length, length), 0)
    scores = jnp.where(masked_out, -jnp.inf, scores)
    peak_score = lax.optimization_barrier(jnp.max(scores, axis=-1, keepdims=True))
    raised = jnp.exp(scores - peak_score)
    shares = raised / lax.optimization_barrier(jnp.sum(raised, axis=-1, keepdims=True))
    shares_low = lax.optimization_barrier(shares.astype(jnp.bfloat16)).astype(jnp.float32)
    output = jnp.einsum('...lm,...md->...ld', shares_low, value_wide).astype(jnp.bfloat16)
    share_grad = jnp.einsum('...ld,...md->...lm', upstream_wide, value_wide)
    value_grad = jnp.einsum('...lm,...ld->...md', shares_low, upstream_wide).astype(jnp.bfloat16)
    row_total = lax.optimization_barrier(jnp.sum(shares * share_grad, axis=-1, keepdims=True))
    score_low = lax.optimization_barrier((shares * (share_grad - row_total)).astype(jnp.bfloat16)).astype(jnp.float32)
    query_grad = (jnp.einsum('...lm,...md->...ld', score_low, key_wide) * factor).astype(jnp.bfloat16)
    key_grad = (jnp.einsum('...lm,...ld->...md', score_low, query_wide) * factor).astype(jnp.bfloat16)
    return (output, query_grad, key_grad, value_grad)

def group_step(grouped):
    return attend_sets(grouped[0], grouped[1], grouped[2], grouped[3])

def reference(queries, keys, values, out_weight, cotangent):
    head_count = ROW_HEADS + COL_HEADS
    head_width = head_count * DH
    flat_cot = cotangent.reshape(-1, D)
    upstream = jnp.dot(flat_cot, out_weight.T, preferred_element_type=jnp.float32).astype(jnp.bfloat16)
    upstream = upstream.reshape(SEQS, ROWS, STRIDE, head_width)
    stacked = [member.reshape(SEQS, ROWS, STRIDE, head_count, DH) for member in (queries, keys, values, upstream)]
    row_parts = tuple((jnp.transpose(member[:, :, :, :ROW_HEADS], (0, 1, 3, 2, 4)).reshape(SEQS * ROWS, ROW_HEADS, STRIDE, DH) for member in stacked))
    row_results = lax.map(group_step, row_parts)
    row_back = [jnp.transpose(member.reshape(SEQS, ROWS, ROW_HEADS, STRIDE, DH), (0, 1, 3, 2, 4)) for member in row_results]
    col_parts = tuple((jnp.transpose(member[:, :, :, ROW_HEADS:], (0, 2, 3, 1, 4)) for member in stacked))
    col_results = lax.map(group_step, col_parts)
    col_back = [jnp.transpose(member, (0, 3, 1, 2, 4)) for member in col_results]
    joined = [jnp.concatenate([first_part, second_part], axis=3).reshape(SEQS, ROWS, STRIDE, head_width) for first_part, second_part in zip(row_back, col_back)]
    attn = joined[0]
    flat_attn = attn.reshape(-1, head_width)
    layer_out = jnp.dot(flat_attn, out_weight, preferred_element_type=jnp.float32).astype(jnp.bfloat16).reshape(SEQS, ROWS, STRIDE, D)
    weight_grad = jnp.dot(flat_attn.T, flat_cot, preferred_element_type=jnp.float32) / math.sqrt(ALL_TOKENS)
    return (layer_out, joined[1], joined[2], joined[3], weight_grad)
```

```python
import functools
import math

import jax
import jax.numpy as jnp
from jax import lax
from jax.experimental import pallas as pl
from jax.experimental.pallas import tpu as pltpu
from jax.sharding import PartitionSpec as P

ROW_HEADS = 4
COL_HEADS = 4
DH = 128
MESH = pl.DeviceIdType.MESH
VMEM_LIMIT = 67000000
PIECES = ((0, 384), (384, 384), (768, 256))
ORDERS = ((2, 1, 0), (1, 0, 2), (0, 2, 1))


def place():
    s = lax.axis_index("seq")
    p = lax.axis_index("dp")
    return (s // 8, (s // 2) % 4, (s % 2) * 2 + p // 2), p % 2


def device(at, core):
    y, x, z = at
    return ((y * 4 + x) * 2 + z // 2, (z % 2) * 2 + core)


def shifted(at, axis, step):
    moved = list(at)
    moved[axis] = (at[axis] + step) % 4
    return tuple(moved)


def greet(seq_peers, ring_peers):
    s = lax.axis_index("seq")
    p = lax.axis_index("dp")
    at, core = place()
    barrier = pltpu.get_barrier_semaphore()
    count = 0
    if seq_peers:

        @pl.loop(1, 32)
        def _(k):
            pl.semaphore_signal(
                barrier, inc=1, device_id=((s + k) % 32, p), device_id_type=MESH
            )

        count += 31
    if ring_peers:
        pl.semaphore_signal(barrier, inc=1, device_id=device(at, 1 - core), device_id_type=MESH)
        count += 1
        for axis in range(3):
            for step in range(1, 4):
                pl.semaphore_signal(
                    barrier,
                    inc=1,
                    device_id=device(shifted(at, axis, step), core),
                    device_id_type=MESH,
                )
                count += 1
    pl.semaphore_wait(barrier, count)


def remote(src, dst, send, recv, to):
    return pltpu.make_async_remote_copy(
        src_ref=src, dst_ref=dst, send_sem=send, recv_sem=recv, device_id=to, device_id_type=MESH
    )


def wait_bytes(ref, sem):
    pltpu.make_async_copy(ref, ref, sem).wait()


def gather_weight(w_ref, pair, full, send, recv, local):
    at, core = place()
    other = device(at, 1 - core)
    swap = remote(w_ref, pair.at[core], send.at[0], recv.at[0], other)
    swap.start()
    own = pltpu.make_async_copy(w_ref, pair.at[core], local)
    own.start()
    own.wait()
    swap.wait()
    half = core * 1024
    own_half = pl.ds(pl.multiple_of(half, 128), 1024)
    full[at[0], at[1], at[2], :, own_half] = jnp.concatenate(
        [pair[0, :, own_half], pair[1, :, own_half]], axis=0
    )
    sem = 1
    for stage in range(3):
        for (start, width), order in zip(PIECES, ORDERS):
            index = tuple(
                pl.ds(0, 4) if axis in order[:stage] else at[axis] for axis in range(3)
            )
            cols = pl.ds(pl.multiple_of(half + start, 128), width)
            region = full.at[index + (slice(None), cols)]
            for step in range(1, 4):
                remote(
                    region,
                    region,
                    send.at[sem],
                    recv.at[sem],
                    device(shifted(at, order[stage], step), core),
                ).start()
            sem += 1
        for k, ((start, width), order) in enumerate(zip(PIECES, ORDERS)):
            index = tuple(
                pl.ds(0, 3)
                if axis == order[stage]
                else (pl.ds(0, 4) if axis in order[:stage] else at[axis])
                for axis in range(3)
            )
            got = full.at[index + (slice(None), pl.ds(0, width))]
            wait_bytes(got, recv.at[sem - 3 + k])
            wait_bytes(got, send.at[sem - 3 + k])
    mine = full.at[:, :, :, :, pl.ds(pl.multiple_of(half, 128), 1024)]
    last = remote(mine, mine, send.at[sem], recv.at[sem], other)
    last.start()
    last.wait()


def gather_kernel(w_ref, out_ref, pair, full, send, recv, local):
    greet(False, True)
    gather_weight(w_ref, pair, full, send, recv, local)
    out = pltpu.make_async_copy(full, out_ref, local)
    out.start()
    out.wait()


def scatter_grad(g_ref, out_ref, bufs, send, recv, factor):
    chip, firsts, seconds, thirds, sums1, sums2, fin, rest = bufs
    at, core = place()
    other = device(at, 1 - core)
    mine = pl.ds(pl.multiple_of(core * 1024, 128), 1024)
    theirs = pl.ds(pl.multiple_of((1 - core) * 1024, 128), 1024)
    swap = remote(g_ref.at[:, :, :, :, theirs], chip, send.at[0], recv.at[0], other)
    swap.start()
    swap.wait()

    @pl.loop(0, 4)
    def _(y):
        @pl.loop(0, 4)
        def _(x):
            total = chip[y, x].astype(jnp.float32) + g_ref[y, x, :, :, mine].astype(jnp.float32)
            chip[y, x] = total.astype(jnp.bfloat16)

    sem = 1
    for stage in range(3):
        for k, ((start, width), order) in enumerate(zip(PIECES, ORDERS)):
            path = order[::-1]
            axis = path[stage]
            left = [a for a in range(3) if a not in path[:stage]]
            for step in range(1, 4):
                to = shifted(at, axis, step)
                index = tuple(to[a] if a == axis else slice(None) for a in left)
                if stage == 0:
                    src = chip.at[index + (slice(None), pl.ds(start, width))]
                    dst = firsts[k].at[step - 1]
                elif stage == 1:
                    src = sums1[k].at[index]
                    dst = seconds[k].at[step - 1]
                else:
                    src = sums2[k].at[index]
                    dst = thirds[k].at[step - 1]
                remote(src, dst, send.at[sem], recv.at[sem], device(to, core)).start()
            sem += 1
        for k, ((start, width), order) in enumerate(zip(PIECES, ORDERS)):
            path = order[::-1]
            axis = path[stage]
            left = [a for a in range(3) if a not in path[:stage]]
            index = tuple(at[a] if a == axis else slice(None) for a in left)
            got = (firsts, seconds, thirds)[stage][k]
            wait_bytes(got, recv.at[sem - 3 + k])
            wait_bytes(got, send.at[sem - 3 + k])
            if stage == 0:
                own = chip[index + (slice(None), pl.ds(start, width))]
            elif stage == 1:
                own = sums1[k][index]
            else:
                own = sums2[k][index]
            total = own.astype(jnp.float32)
            for step in range(3):
                total = total + got[step].astype(jnp.float32)
            if stage == 0:
                sums1[k][...] = total.astype(jnp.bfloat16)
            elif stage == 1:
                sums2[k][...] = total.astype(jnp.bfloat16)
            else:
                for low in range(2):
                    fin[low, :, pl.ds(start, width)] = total[low * 8 : low * 8 + 8] * factor
    last = remote(fin.at[1 - core], rest, send.at[sem], recv.at[sem], other)
    last.start()
    last.wait()
    out_ref[:, mine] = fin[core]
    out_ref[:, theirs] = rest[...]


def scatter_bufs():
    def three(*lead):
        return [pltpu.VMEM(lead + (width,), jnp.bfloat16) for _, width in PIECES]

    return [
        pltpu.VMEM((4, 4, 4, 16, 1024), jnp.bfloat16),
        three(3, 4, 4, 16),
        three(3, 4, 16),
        three(3, 16),
        three(4, 4, 16),
        three(4, 16),
        pltpu.VMEM((2, 8, 1024), jnp.float32),
        pltpu.VMEM((8, 1024), jnp.float32),
    ]


def scatter_kernel(factor, g_ref, out_ref, bufs, send, recv):
    greet(False, True)
    scatter_grad(g_ref, out_ref, bufs, send, recv, factor)


def exchange_kernel(count, forward, *refs):
    xs, outs = refs[:count], refs[count : 2 * count]
    send, recv, local = refs[2 * count :]
    s = lax.axis_index("seq")
    p = lax.axis_index("dp")
    greet(True, False)
    half = pl.ds(512, 512)

    def src(t, q):
        return xs[t].at[pl.ds(q * 32, 32), half] if forward else xs[t].at[q]

    def dst(t):
        return outs[t].at[s] if forward else outs[t].at[pl.ds(s * 32, 32)]

    def some(t):
        return outs[t].at[pl.ds(0, 31)] if forward else outs[t].at[pl.ds(0, 31 * 32)]

    for t in range(count):

        @pl.loop(1, 32)
        def _(k):
            q = (s + k) % 32
            remote(src(t, q), dst(t), send.at[t], recv.at[t], (q, p)).start()

        pltpu.make_async_copy(src(t, s), dst(t), local.at[t]).start()
    for t in range(count):
        pltpu.make_async_copy(src(t, s), dst(t), local.at[t]).wait()
        wait_bytes(some(t), recv.at[t])
        wait_bytes(some(t), send.at[t])


ANY = pl.BlockSpec(memory_space=pl.ANY)
INV = pl.BlockSpec(memory_space=pltpu.VMEM)


def params(collective_id):
    return pltpu.CompilerParams(
        collective_id=collective_id, has_side_effects=True, vmem_limit_bytes=VMEM_LIMIT
    )


def all_weight(out_weight):
    full = pl.pallas_call(
        gather_kernel,
        out_shape=jax.ShapeDtypeStruct((4, 4, 4, 16, 2048), jnp.bfloat16),
        in_specs=[ANY],
        out_specs=ANY,
        scratch_shapes=[
            pltpu.VMEM((2, 8, 2048), jnp.bfloat16),
            pltpu.VMEM((4, 4, 4, 16, 2048), jnp.bfloat16),
            pltpu.SemaphoreType.DMA((11,)),
            pltpu.SemaphoreType.DMA((11,)),
            pltpu.SemaphoreType.DMA,
        ],
        compiler_params=params(1),
    )(out_weight)
    return full.reshape(1024, 2048)


def summed_grad(grad, factor):
    return pl.pallas_call(
        functools.partial(scatter_kernel, factor),
        out_shape=jax.ShapeDtypeStruct((8, 2048), jnp.float32),
        in_specs=[INV],
        out_specs=INV,
        scratch_shapes=[
            scatter_bufs(),
            pltpu.SemaphoreType.DMA((11,)),
            pltpu.SemaphoreType.DMA((11,)),
        ],
        compiler_params=params(2),
    )(grad.reshape(4, 4, 4, 16, 2048))


def exchange(arrays, forward, collective_id):
    shape = (32, 32, 512) if forward else (1024, 512)
    return pl.pallas_call(
        functools.partial(exchange_kernel, len(arrays), forward),
        out_shape=[jax.ShapeDtypeStruct(shape, jnp.bfloat16)] * len(arrays),
        in_specs=[ANY] * len(arrays),
        out_specs=[ANY] * len(arrays),
        scratch_shapes=[pltpu.SemaphoreType.DMA((len(arrays),))] * 3,
        compiler_params=params(collective_id),
    )(*arrays)


def attend_sets(query_set, key_set, value_set, upstream_set):
    factor = 1.0 / math.sqrt(query_set.shape[-1])
    scores = (
        jnp.einsum("...ld,...md->...lm", query_set, key_set, preferred_element_type=jnp.float32)
        * factor
    )
    length = scores.shape[-1]
    masked_out = lax.broadcasted_iota(jnp.int32, (length, length), 1) > lax.broadcasted_iota(
        jnp.int32, (length, length), 0
    )
    scores = jnp.where(masked_out, -jnp.inf, scores)
    peak_score = jnp.max(scores, axis=-1, keepdims=True)
    raised = jnp.exp(scores - peak_score)
    shares = raised / jnp.sum(raised, axis=-1, keepdims=True)
    shares_low = shares.astype(jnp.bfloat16)
    output = jnp.einsum(
        "...lm,...md->...ld", shares_low, value_set, preferred_element_type=jnp.float32
    ).astype(jnp.bfloat16)
    share_grad = jnp.einsum(
        "...ld,...md->...lm", upstream_set, value_set, preferred_element_type=jnp.float32
    )
    value_grad = jnp.einsum(
        "...lm,...ld->...md", shares_low, upstream_set, preferred_element_type=jnp.float32
    ).astype(jnp.bfloat16)
    row_total = jnp.sum(shares * share_grad, axis=-1, keepdims=True)
    score_low = (shares * (share_grad - row_total)).astype(jnp.bfloat16)
    query_grad = (
        jnp.einsum("...lm,...md->...ld", score_low, key_set, preferred_element_type=jnp.float32)
        * factor
    ).astype(jnp.bfloat16)
    key_grad = (
        jnp.einsum("...lm,...ld->...md", score_low, query_set, preferred_element_type=jnp.float32)
        * factor
    ).astype(jnp.bfloat16)
    return (output, query_grad, key_grad, value_grad)


def body(queries, keys, values, out_weight, cotangent):
    flat = [member.reshape(1024, 1024) for member in (queries, keys, values)]
    flat_cot = cotangent.reshape(1024, 2048)
    weight_full = all_weight(out_weight)
    upstream = jnp.einsum(
        "td,hd->th", flat_cot, weight_full, preferred_element_type=jnp.float32
    ).astype(jnp.bfloat16)
    members = flat + [upstream]
    columns = exchange(members, True, 3)
    columns = [jnp.moveaxis(member.reshape(32, 32, 4, 128), 0, 2) for member in columns]
    column_results = attend_sets(*columns)
    returned = exchange(
        [jnp.moveaxis(member, 2, 0).reshape(32, 32, 512) for member in column_results], False, 4
    )
    row_results = lax.map(
        lambda group: attend_sets(*group),
        tuple(
            jnp.moveaxis(member[:, :512].reshape(1024, 4, 128), 1, 0) for member in members
        ),
    )
    joined = [
        jnp.concatenate([jnp.moveaxis(row, 0, 1).reshape(1024, 512), col], axis=-1)
        for row, col in zip(row_results, returned)
    ]
    attn = joined[0]
    layer_out = jnp.dot(attn, weight_full, preferred_element_type=jnp.float32).astype(jnp.bfloat16)
    grad = jnp.einsum("th,td->hd", attn, flat_cot, preferred_element_type=jnp.float32)
    weight_grad = summed_grad(grad.astype(jnp.bfloat16), 1.0 / math.sqrt(4 * 32 * 1024))
    return (
        layer_out.reshape(1, 1, 1024, 2048),
        joined[1].reshape(1, 1, 1024, 1024),
        joined[2].reshape(1, 1, 1024, 1024),
        joined[3].reshape(1, 1, 1024, 1024),
        weight_grad,
    )


def solution(mesh):
    return jax.shard_map(
        body,
        mesh=mesh,
        in_specs=(
            P("dp", "seq", None, None),
            P("dp", "seq", None, None),
            P("dp", "seq", None, None),
            P(("seq", "dp"), None),
            P("dp", "seq", None, None),
        ),
        out_specs=(
            P("dp", "seq", None, None),
            P("dp", "seq", None, None),
            P("dp", "seq", None, None),
            P("dp", "seq", None, None),
            P(("seq", "dp"), None),
        ),
        check_vma=False,
    )
```

```python
import functools
import math

import jax
import jax.numpy as jnp
from jax import lax
from jax.experimental import pallas as pl
from jax.experimental.pallas import tpu as pltpu
from jax.sharding import PartitionSpec as P

ROW_HEADS = 4
COL_HEADS = 4
DH = 128
MESH = pl.DeviceIdType.MESH
VMEM_LIMIT = 67000000
PIECES = ((0, 384), (384, 384), (768, 256))
ORDERS = ((2, 1, 0), (1, 0, 2), (0, 2, 1))


def place():
    s = lax.axis_index("seq")
    p = lax.axis_index("dp")
    return (s // 8, (s // 2) % 4, (s % 2) * 2 + p // 2), p % 2


def device(at, core):
    y, x, z = at
    return ((y * 4 + x) * 2 + z // 2, (z % 2) * 2 + core)


def shifted(at, axis, step):
    moved = list(at)
    moved[axis] = (at[axis] + step) % 4
    return tuple(moved)


def greet(seq_peers, ring_peers):
    s = lax.axis_index("seq")
    p = lax.axis_index("dp")
    at, core = place()
    barrier = pltpu.get_barrier_semaphore()
    count = 0
    if seq_peers:

        @pl.loop(1, 32)
        def _(k):
            pl.semaphore_signal(
                barrier, inc=1, device_id=((s + k) % 32, p), device_id_type=MESH
            )

        count += 31
    if ring_peers:
        pl.semaphore_signal(barrier, inc=1, device_id=device(at, 1 - core), device_id_type=MESH)
        count += 1
        for axis in range(3):
            for step in range(1, 4):
                pl.semaphore_signal(
                    barrier,
                    inc=1,
                    device_id=device(shifted(at, axis, step), core),
                    device_id_type=MESH,
                )
                count += 1
    pl.semaphore_wait(barrier, count)


def remote(src, dst, send, recv, to):
    return pltpu.make_async_remote_copy(
        src_ref=src, dst_ref=dst, send_sem=send, recv_sem=recv, device_id=to, device_id_type=MESH
    )


def wait_bytes(ref, sem):
    pltpu.make_async_copy(ref, ref, sem).wait()


def gather_start(w_ref, pair, full, send, recv, local):
    at, core = place()
    swap = remote(w_ref, pair.at[core], send.at[0], recv.at[0], device(at, 1 - core))
    swap.start()
    own = pltpu.make_async_copy(w_ref, pair.at[core], local)
    own.start()
    own.wait()
    swap.wait()
    half = pl.ds(pl.multiple_of(core * 1024, 128), 1024)
    full[at[0], at[1], at[2], :, half] = jnp.concatenate(
        [pair[0, :, half], pair[1, :, half]], axis=0
    )


def gather_send(stage, full, send, recv):
    at, core = place()
    for k, ((start, width), order) in enumerate(zip(PIECES, ORDERS)):
        index = tuple(pl.ds(0, 4) if axis in order[:stage] else at[axis] for axis in range(3))
        cols = pl.ds(pl.multiple_of(core * 1024 + start, 128), width)
        region = full.at[index + (slice(None), cols)]
        for step in range(1, 4):
            to = device(shifted(at, order[stage], step), core)
            sem = 1 + 3 * stage + k
            remote(region, region, send.at[sem], recv.at[sem], to).start()


def gather_wait(stage, full, sems):
    at, core = place()
    for k, ((start, width), order) in enumerate(zip(PIECES, ORDERS)):
        index = tuple(
            pl.ds(0, 3)
            if axis == order[stage]
            else (pl.ds(0, 4) if axis in order[:stage] else at[axis])
            for axis in range(3)
        )
        wait_bytes(full.at[index + (slice(None), pl.ds(0, width))], sems.at[1 + 3 * stage + k])


def gather_last(full, send, recv):
    at, core = place()
    mine = full.at[:, :, :, :, pl.ds(pl.multiple_of(core * 1024, 128), 1024)]
    return remote(mine, mine, send.at[10], recv.at[10], device(at, 1 - core))


def scatter_grad(g_ref, out_ref, bufs, send, recv, factor, meanwhile):
    chip, firsts, seconds, thirds, sums1, sums2, fin, rest = bufs
    at, core = place()
    other = device(at, 1 - core)
    mine = pl.ds(pl.multiple_of(core * 1024, 128), 1024)
    theirs = pl.ds(pl.multiple_of((1 - core) * 1024, 128), 1024)
    swap = remote(g_ref.at[:, :, :, :, theirs], chip, send.at[0], recv.at[0], other)
    swap.start()
    swap.wait_recv()

    @pl.loop(0, 4)
    def _(y):
        @pl.loop(0, 4)
        def _(x):
            total = chip[y, x].astype(jnp.float32) + g_ref[y, x, :, :, mine].astype(jnp.float32)
            chip[y, x] = total.astype(jnp.bfloat16)

    sem = 1
    for stage in range(3):
        for k, ((start, width), order) in enumerate(zip(PIECES, ORDERS)):
            path = order[::-1]
            axis = path[stage]
            left = [a for a in range(3) if a not in path[:stage]]
            for step in range(1, 4):
                to = shifted(at, axis, step)
                index = tuple(to[a] if a == axis else slice(None) for a in left)
                if stage == 0:
                    src = chip.at[index + (slice(None), pl.ds(start, width))]
                    dst = firsts[k].at[step - 1]
                elif stage == 1:
                    src = sums1[k].at[index]
                    dst = seconds[k].at[step - 1]
                else:
                    src = sums2[k].at[index]
                    dst = thirds[k].at[step - 1]
                remote(src, dst, send.at[sem], recv.at[sem], device(to, core)).start()
            sem += 1
        if stage == 0:
            meanwhile()
            swap.wait_send()
        for k, ((start, width), order) in enumerate(zip(PIECES, ORDERS)):
            path = order[::-1]
            axis = path[stage]
            left = [a for a in range(3) if a not in path[:stage]]
            index = tuple(at[a] if a == axis else slice(None) for a in left)
            got = (firsts, seconds, thirds)[stage][k]
            wait_bytes(got, recv.at[sem - 3 + k])
            wait_bytes(got, send.at[sem - 3 + k])
            if stage == 0:
                own = chip[index + (slice(None), pl.ds(start, width))]
            elif stage == 1:
                own = sums1[k][index]
            else:
                own = sums2[k][index]
            total = own.astype(jnp.float32)
            for step in range(3):
                total = total + got[step].astype(jnp.float32)
            if stage == 0:
                sums1[k][...] = total.astype(jnp.bfloat16)
            elif stage == 1:
                sums2[k][...] = total.astype(jnp.bfloat16)
            else:
                for low in range(2):
                    fin[low, :, pl.ds(start, width)] = total[low * 8 : low * 8 + 8] * factor
    last = remote(fin.at[1 - core], rest, send.at[sem], recv.at[sem], other)
    last.start()
    last.wait()
    out_ref[:, mine] = fin[core]
    out_ref[:, theirs] = rest[...]


def scatter_bufs():
    def three(*lead):
        return [pltpu.VMEM(lead + (width,), jnp.bfloat16) for _, width in PIECES]

    return [
        pltpu.VMEM((4, 4, 4, 16, 1024), jnp.bfloat16),
        three(3, 4, 4, 16),
        three(3, 4, 16),
        three(3, 16),
        three(4, 4, 16),
        three(4, 16),
        pltpu.VMEM((2, 8, 1024), jnp.float32),
        pltpu.VMEM((8, 1024), jnp.float32),
    ]


def scatter_bufs():
    def three(*lead):
        return [pltpu.VMEM(lead + (width,), jnp.bfloat16) for _, width in PIECES]

    return [
        pltpu.VMEM((4, 4, 4, 16, 1024), jnp.bfloat16),
        three(3, 4, 4, 16),
        three(3, 4, 16),
        three(3, 16),
        three(4, 4, 16),
        three(4, 16),
        pltpu.VMEM((2, 8, 1024), jnp.float32),
        pltpu.VMEM((8, 1024), jnp.float32),
    ]


SCALE = 1.0 / math.sqrt(DH)
EXP2_SCALE = SCALE * math.log2(math.e)


def dot(a, b):
    return jnp.dot(a, b, preferred_element_type=jnp.float32)


def dot_nt(a, b):
    return lax.dot_general(a, b, (((1,), (1,)), ((), ())), preferred_element_type=jnp.float32)


def low(a):
    return a.astype(jnp.bfloat16)


def softmax_blocks(query, key_blocks, biases):
    scores = [dot_nt(key, query) for key in key_blocks]
    scores = [s if b is None else s + b for s, b in zip(scores, biases)]
    peak = functools.reduce(
        jnp.maximum, [jnp.max(s, axis=0, keepdims=True) for s in scores]
    )
    raised = [jnp.exp2((s - peak) * EXP2_SCALE) for s in scores]
    inverse = 1.0 / sum(jnp.sum(r, axis=0, keepdims=True) for r in raised)
    return [r * inverse for r in raised]


def score_grads(shares, value_blocks, upstream):
    grads = [dot_nt(value, upstream) for value in value_blocks]
    total = sum(jnp.sum(s * g, axis=0, keepdims=True) for s, g in zip(shares, grads))
    return [low(s * (g - total)) for s, g in zip(shares, grads)]


def row_head(head, qr, kr, vr, ur, attn, attn_t, dq, dk, dv, bias, key_t, value_t, dk_acc, dv_acc):
    lanes = pl.ds(pl.multiple_of(head * DH, DH), DH)
    key_t[...] = kr[:, lanes].T
    value_t[...] = vr[:, lanes].T
    for i in range(4):
        here = pl.ds(i * 256, 256)
        query, upstream = qr[here, lanes], ur[here, lanes]
        spans = [pl.ds(j * 256, 256) for j in range(i + 1)]
        shares = softmax_blocks(
            query, [kr[span, lanes] for span in spans], [None] * i + [bias[0]]
        )
        lows = [low(share) for share in shares]
        out_t = low(sum(dot(value_t[:, span], share) for span, share in zip(spans, lows)))
        attn_t[pl.ds(pl.multiple_of(head * DH, DH), DH), here] = out_t
        attn[here, lanes] = out_t.T
        grads = score_grads(shares, [vr[span, lanes] for span in spans], upstream)
        for j, span in enumerate(spans):
            to_value, to_key = dot(lows[j], upstream), dot(grads[j], query)
            if j == i:
                dv_acc[span] = to_value
                dk_acc[span] = to_key
            else:
                dv_acc[span] += to_value
                dk_acc[span] += to_key
        to_query = sum(dot(key_t[:, span], grad) for span, grad in zip(spans, grads))
        dq[here, lanes] = low(to_query.T * SCALE)
    dk[:, lanes] = low(dk_acc[...] * SCALE)
    dv[:, lanes] = low(dv_acc[...])


def column_block(ref, half, group, lanes):
    return ref[pl.ds(half * 16, 16), pl.ds(group, 16), lanes].reshape(256, DH)


def put_column(ref, half, group, lanes, block):
    ref[pl.ds(half * 16, 16), pl.ds(group, 16), lanes] = low(block).reshape(16, 16, DH)


def column_place(unit):
    group = pl.multiple_of((unit // 4) * 16, 16)
    return group, pl.ds(pl.multiple_of((unit % 4) * DH, DH), DH)


def column_forward(unit, cin, cout, bias, kept):
    group, lanes = column_place(unit)
    key = [column_block(cin[1], half, group, lanes) for half in range(2)]
    value_t = [column_block(cin[2], half, group, lanes).T for half in range(2)]
    slot = 0
    for i in range(2):
        query = column_block(cin[0], i, group, lanes)
        shares = softmax_blocks(query, key[: i + 1], [bias[1]] * i + [bias[2]])
        for share in shares:
            kept[unit, slot] = share
            slot += 1
        out_t = sum(dot(value_t[j], low(share)) for j, share in enumerate(shares))
        put_column(cout[0], i, group, lanes, out_t.T)


def column_backward(unit, cin, cout, kept):
    group, lanes = column_place(unit)
    key = [column_block(cin[1], half, group, lanes) for half in range(2)]
    key_t = [block.T for block in key]
    value = [column_block(cin[2], half, group, lanes) for half in range(2)]
    to_key, to_value = [0.0, 0.0], [0.0, 0.0]
    slot = 0
    for i in range(2):
        query = column_block(cin[0], i, group, lanes)
        upstream = column_block(cin[3], i, group, lanes)
        shares = [kept[unit, slot + j] for j in range(i + 1)]
        slot += i + 1
        grads = score_grads(shares, value[: i + 1], upstream)
        for j in range(i + 1):
            to_value[j] = to_value[j] + dot(low(shares[j]), upstream)
            to_key[j] = to_key[j] + dot(grads[j], query)
        to_query = sum(dot(key_t[j], grad) for j, grad in enumerate(grads))
        put_column(cout[1], i, group, lanes, to_query.T * SCALE)
    for j in range(2):
        put_column(cout[2], j, group, lanes, to_key[j] * SCALE)
        put_column(cout[3], j, group, lanes, to_value[j])


def mega_kernel(factor, *refs):
    q_in, k_in, v_in, w_in, cot_in = refs[:5]
    out_hbm, dq_hbm, dk_hbm, dv_hbm, grad_out = refs[5:10]
    (
        pair,
        full,
        cot,
        rows_in,
        u_row,
        u_col,
        cin,
        cout,
        attn,
        attn_t,
        rows_out,
        accs,
        trans,
        grad,
        layer,
        bias,
        kept,
        bufs,
        ag_send,
        ag_recv,
        rs_send,
        rs_recv,
        go_send,
        go_recv,
        go_local,
        back_send,
        back_recv,
        back_local,
        load,
        store,
    ) = refs[10:]
    s = lax.axis_index("seq")
    p = lax.axis_index("dp")
    row_half, col_half = pl.ds(0, 512), pl.ds(512, 512)
    loads = [pltpu.make_async_copy(cot_in, cot, load.at[0])] + [
        pltpu.make_async_copy(src.at[:, row_half], dst, load.at[1 + t])
        for t, (src, dst) in enumerate(zip((q_in, k_in, v_in), rows_in))
    ]
    for copy in loads:
        copy.start()

    def go_src(t, to):
        if t == 3:
            return u_col.at[pl.ds(to * 32, 32)]
        return (q_in, k_in, v_in)[t].at[pl.ds(to * 32, 32), col_half]

    def go_start(t):
        @pl.loop(1, 32)
        def _(k):
            to = (s + k) % 32
            remote(go_src(t, to), cin[t].at[s], go_send.at[t], go_recv.at[t], (to, p)).start()

        pltpu.make_async_copy(go_src(t, s), cin[t].at[s], go_local.at[t]).start()

    def go_wait(t):
        pltpu.make_async_copy(go_src(t, s), cin[t].at[s], go_local.at[t]).wait()
        wait_bytes(cin[t].at[pl.ds(0, 31)], go_recv.at[t])

    def back_dst(t):
        whole = (attn, dq_hbm, dk_hbm, dv_hbm)[t]
        return whole.at[pl.ds(s * 32, 32), col_half]

    def back_start(t):
        @pl.loop(1, 32)
        def _(k):
            to = (s + k) % 32
            remote(cout[t].at[to], back_dst(t), back_send.at[t], back_recv.at[t], (to, p)).start()

        pltpu.make_async_copy(cout[t].at[s], back_dst(t), back_local.at[t]).start()

    def back_wait(t):
        pltpu.make_async_copy(cout[t].at[s], back_dst(t), back_local.at[t]).wait()
        wait_bytes(cout[t].at[pl.ds(0, 31)], back_recv.at[t])

    greet(True, True)
    gather_start(w_in, pair, full, ag_send, ag_recv, load.at[4])
    gather_send(0, full, ag_send, ag_recv)
    lane = lax.broadcasted_iota(jnp.int32, (256, 256), 1)
    sub = lax.broadcasted_iota(jnp.int32, (256, 256), 0)
    same = lane % 16 == sub % 16
    bias[0] = jnp.where(sub <= lane, 0.0, -jnp.inf)
    bias[1] = jnp.where(same, 0.0, -jnp.inf)
    bias[2] = jnp.where(same & (sub <= lane), 0.0, -jnp.inf)
    gather_wait(0, full, ag_recv)
    gather_send(1, full, ag_send, ag_recv)
    gather_wait(1, full, ag_recv)
    gather_send(2, full, ag_send, ag_recv)
    for t in (1, 0, 2):
        go_start(t)
    gather_wait(2, full, ag_recv)
    last = gather_last(full, ag_send, ag_recv)
    last.start()
    last.wait_recv()
    loads[0].wait()

    def upstream_part(y, dst):
        weight = full.at[y]
        place_at = (y % 2) * 256

        @pl.loop(0, 2)
        def _(block):
            here = pl.ds(pl.multiple_of(block * 512, 512), 512)
            dst[here, pl.ds(place_at, 256)] = low(
                dot_nt(cot[here, :], weight[...].reshape(256, 2048))
            )

    upstream_part(2, u_col)
    upstream_part(3, u_col)
    go_start(3)
    upstream_part(0, u_row)
    upstream_part(1, u_row)
    for copy in loads[1:]:
        copy.wait()

    def row_heads(first, end):
        @pl.loop(first, end)
        def _(head):
            row_head(head, *rows_in, u_row, attn, attn_t, *rows_out, bias, *trans, *accs)

    row_heads(0, 2)
    for t in range(3):
        go_wait(t)

    @pl.loop(0, 8)
    def _(unit):
        column_forward(unit, cin, cout, bias, kept)

    back_start(0)
    row_heads(2, 3)
    go_wait(3)

    @pl.loop(0, 8)
    def _(unit):
        column_backward(unit, cin, cout, kept)

    for t in (3, 2, 1):
        back_start(t)
    row_heads(3, 4)
    row_stores = [
        pltpu.make_async_copy(src, dst.at[:, row_half], store.at[t])
        for t, (src, dst) in enumerate(zip(rows_out, (dq_hbm, dk_hbm, dv_hbm)))
    ]
    for copy in row_stores:
        copy.start()

    def grad_part(half):
        @pl.loop(0, 8)
        def _(block):
            cols = pl.ds(pl.multiple_of(block * 256, 256), 256)
            part = dot(attn_t[pl.ds(half * 512, 512), :], cot[:, cols])
            grad[pl.ds(half * 2, 2), :, :, :, cols] = low(part).reshape(2, 4, 4, 16, 256)

    grad_part(0)
    back_wait(0)

    @pl.loop(0, 4)
    def _(block):
        here = pl.ds(pl.multiple_of(block * 256, 256), 256)
        attn_t[pl.ds(512, 512), here] = attn[here, col_half].T

    grad_part(1)

    def project():
        @pl.loop(0, 8)
        def _(block):
            cols = pl.ds(pl.multiple_of(block * 256, 256), 256)
            layer[:, cols] = low(dot(attn[...], full[:, :, :, :, cols].reshape(1024, 256)))
            pltpu.make_async_copy(layer.at[:, cols], out_hbm.at[:, cols], store.at[3]).start()

    scatter_grad(grad, grad_out, bufs, rs_send, rs_recv, factor, project)
    pltpu.make_async_copy(layer, out_hbm, store.at[3]).wait()
    for copy in row_stores:
        copy.wait()
    for stage in range(3):
        gather_wait(stage, full, ag_send)
    last.wait_send()
    for t in (3, 2, 1):
        back_wait(t)
    for t in range(4):
        wait_bytes(cout[t].at[pl.ds(0, 31)], back_send.at[t])
        wait_bytes(cin[t].at[pl.ds(0, 31)], go_send.at[t])


ANY = pl.BlockSpec(memory_space=pl.ANY)
INV = pl.BlockSpec(memory_space=pltpu.VMEM)


def body(queries, keys, values, out_weight, cotangent):
    def vmem(*shape, dtype=jnp.bfloat16):
        return pltpu.VMEM(shape, dtype)

    def dma(count):
        return pltpu.SemaphoreType.DMA((count,))

    half = [1024, 512]
    shapes = [(1024, 2048), (1024, 1024), (1024, 1024), (1024, 1024)]
    results = pl.pallas_call(
        functools.partial(mega_kernel, 1.0 / math.sqrt(4 * 32 * 1024)),
        out_shape=[jax.ShapeDtypeStruct(shape, jnp.bfloat16) for shape in shapes]
        + [jax.ShapeDtypeStruct((8, 2048), jnp.float32)],
        in_specs=[ANY] * 5,
        out_specs=[ANY] * 4 + [INV],
        scratch_shapes=[
            vmem(2, 8, 2048),
            vmem(4, 4, 4, 16, 2048),
            vmem(1024, 2048),
            [vmem(*half) for _ in range(3)],
            vmem(*half),
            vmem(*half),
            [vmem(32, 32, 512) for _ in range(4)],
            [vmem(32, 32, 512) for _ in range(4)],
            vmem(1024, 1024),
            vmem(1024, 1024),
            [vmem(*half) for _ in range(3)],
            [vmem(1024, DH, dtype=jnp.float32) for _ in range(2)],
            [vmem(DH, 1024) for _ in range(2)],
            vmem(4, 4, 4, 16, 2048),
            vmem(1024, 2048),
            vmem(3, 256, 256, dtype=jnp.float32),
            vmem(8, 3, 256, 256, dtype=jnp.float32),
            scatter_bufs(),
            dma(11),
            dma(11),
            dma(11),
            dma(11),
            dma(4),
            dma(4),
            dma(4),
            dma(4),
            dma(4),
            dma(4),
            dma(5),
            dma(4),
        ],
        compiler_params=pltpu.CompilerParams(
            collective_id=1, has_side_effects=True, vmem_limit_bytes=VMEM_LIMIT
        ),
    )(
        *[member.reshape(1024, 1024) for member in (queries, keys, values)],
        out_weight,
        cotangent.reshape(1024, 2048),
    )
    return (
        results[0].reshape(1, 1, 1024, 2048),
        results[1].reshape(1, 1, 1024, 1024),
        results[2].reshape(1, 1, 1024, 1024),
        results[3].reshape(1, 1, 1024, 1024),
        results[4],
    )


def solution(mesh):
    return jax.shard_map(
        body,
        mesh=mesh,
        in_specs=(
            P("dp", "seq", None, None),
            P("dp", "seq", None, None),
            P("dp", "seq", None, None),
            P(("seq", "dp"), None),
            P("dp", "seq", None, None),
        ),
        out_specs=(
            P("dp", "seq", None, None),
            P("dp", "seq", None, None),
            P("dp", "seq", None, None),
            P("dp", "seq", None, None),
            P(("seq", "dp"), None),
        ),
        check_vma=False,
    )
```

```python
import functools
import math

import jax
import jax.numpy as jnp
from jax import lax
from jax.experimental import pallas as pl
from jax.experimental.pallas import tpu as pltpu
from jax.sharding import PartitionSpec as P

ROW_HEADS = 4
COL_HEADS = 4
DH = 128
MESH = pl.DeviceIdType.MESH
VMEM_LIMIT = 67000000
PIECES = ((0, 384), (384, 384), (768, 256))
ORDERS = ((2, 1, 0), (1, 0, 2), (0, 2, 1))


def place():
    s = lax.axis_index("seq")
    p = lax.axis_index("dp")
    return (s // 8, (s // 2) % 4, (s % 2) * 2 + p // 2), p % 2


def device(at, core):
    y, x, z = at
    return ((y * 4 + x) * 2 + z // 2, (z % 2) * 2 + core)


def shifted(at, axis, step):
    moved = list(at)
    moved[axis] = (at[axis] + step) % 4
    return tuple(moved)


def greet(seq_peers, ring_peers):
    s = lax.axis_index("seq")
    p = lax.axis_index("dp")
    at, core = place()
    barrier = pltpu.get_barrier_semaphore()
    count = 0
    if seq_peers:

        @pl.loop(1, 32)
        def _(k):
            pl.semaphore_signal(
                barrier, inc=1, device_id=((s + k) % 32, p), device_id_type=MESH
            )

        count += 31
    if ring_peers:
        pl.semaphore_signal(barrier, inc=1, device_id=device(at, 1 - core), device_id_type=MESH)
        count += 1
        for axis in range(3):
            for step in range(1, 4):
                pl.semaphore_signal(
                    barrier,
                    inc=1,
                    device_id=device(shifted(at, axis, step), core),
                    device_id_type=MESH,
                )
                count += 1
    pl.semaphore_wait(barrier, count)


def remote(src, dst, send, recv, to):
    return pltpu.make_async_remote_copy(
        src_ref=src, dst_ref=dst, send_sem=send, recv_sem=recv, device_id=to, device_id_type=MESH
    )


def wait_bytes(ref, sem):
    pltpu.make_async_copy(ref, ref, sem).wait()


def gather_start(w_ref, pair, full, send, recv, local):
    at, core = place()
    swap = remote(w_ref, pair.at[core], send.at[0], recv.at[0], device(at, 1 - core))
    swap.start()
    own = pltpu.make_async_copy(w_ref, pair.at[core], local)
    own.start()
    own.wait()
    swap.wait()
    half = pl.ds(pl.multiple_of(core * 1024, 128), 1024)
    full[at[0], at[1], at[2], :, half] = jnp.concatenate(
        [pair[0, :, half], pair[1, :, half]], axis=0
    )


def gather_send(stage, full, send, recv):
    at, core = place()
    for k, ((start, width), order) in enumerate(zip(PIECES, ORDERS)):
        index = tuple(pl.ds(0, 4) if axis in order[:stage] else at[axis] for axis in range(3))
        cols = pl.ds(pl.multiple_of(core * 1024 + start, 128), width)
        region = full.at[index + (slice(None), cols)]
        for step in range(1, 4):
            to = device(shifted(at, order[stage], step), core)
            sem = 1 + 3 * stage + k
            remote(region, region, send.at[sem], recv.at[sem], to).start()


def gather_wait(stage, full, sems):
    at, core = place()
    for k, ((start, width), order) in enumerate(zip(PIECES, ORDERS)):
        index = tuple(
            pl.ds(0, 3)
            if axis == order[stage]
            else (pl.ds(0, 4) if axis in order[:stage] else at[axis])
            for axis in range(3)
        )
        wait_bytes(full.at[index + (slice(None), pl.ds(0, width))], sems.at[1 + 3 * stage + k])


def gather_last(full, send, recv):
    at, core = place()
    mine = full.at[:, :, :, :, pl.ds(pl.multiple_of(core * 1024, 128), 1024)]
    return remote(mine, mine, send.at[10], recv.at[10], device(at, 1 - core))


def swap_start(half, g_ref, chip, send, recv):
    at, core = place()
    rows = pl.ds(half * 2, 2)
    theirs = pl.ds(pl.multiple_of((1 - core) * 1024, 128), 1024)
    src = g_ref.at[rows, :, :, :, theirs]
    remote(src, chip.at[rows], send.at[0], recv.at[0], device(at, 1 - core)).start()


def scatter_grad(g_ref, out_ref, bufs, send, recv, factor, meanwhile):
    chip, firsts, seconds, thirds, sums1, sums2, fin, rest = bufs
    at, core = place()
    other = device(at, 1 - core)
    mine = pl.ds(pl.multiple_of(core * 1024, 128), 1024)
    theirs = pl.ds(pl.multiple_of((1 - core) * 1024, 128), 1024)
    wait_bytes(chip, recv.at[0])

    @pl.loop(0, 4)
    def _(y):
        @pl.loop(0, 4)
        def _(x):
            total = chip[y, x].astype(jnp.float32) + g_ref[y, x, :, :, mine].astype(jnp.float32)
            chip[y, x] = total.astype(jnp.bfloat16)

    sem = 1
    for stage in range(3):
        for k, ((start, width), order) in enumerate(zip(PIECES, ORDERS)):
            path = order[::-1]
            axis = path[stage]
            left = [a for a in range(3) if a not in path[:stage]]
            for step in range(1, 4):
                to = shifted(at, axis, step)
                index = tuple(to[a] if a == axis else slice(None) for a in left)
                if stage == 0:
                    src = chip.at[index + (slice(None), pl.ds(start, width))]
                    dst = firsts[k].at[step - 1]
                elif stage == 1:
                    src = sums1[k].at[index]
                    dst = seconds[k].at[step - 1]
                else:
                    src = sums2[k].at[index]
                    dst = thirds[k].at[step - 1]
                remote(src, dst, send.at[sem], recv.at[sem], device(to, core)).start()
            sem += 1
        meanwhile(stage)
        for k, ((start, width), order) in enumerate(zip(PIECES, ORDERS)):
            path = order[::-1]
            axis = path[stage]
            left = [a for a in range(3) if a not in path[:stage]]
            index = tuple(at[a] if a == axis else slice(None) for a in left)
            got = (firsts, seconds, thirds)[stage][k]
            wait_bytes(got, recv.at[sem - 3 + k])
            wait_bytes(got, send.at[sem - 3 + k])
            if stage == 0:
                own = chip[index + (slice(None), pl.ds(start, width))]
            elif stage == 1:
                own = sums1[k][index]
            else:
                own = sums2[k][index]
            total = own.astype(jnp.float32)
            for step in range(3):
                total = total + got[step].astype(jnp.float32)
            if stage == 0:
                sums1[k][...] = total.astype(jnp.bfloat16)
            elif stage == 1:
                sums2[k][...] = total.astype(jnp.bfloat16)
            else:
                for low in range(2):
                    fin[low, :, pl.ds(start, width)] = total[low * 8 : low * 8 + 8] * factor
    last = remote(fin.at[1 - core], rest, send.at[sem], recv.at[sem], other)
    last.start()
    last.wait()
    wait_bytes(chip, send.at[0])
    out_ref[:, mine] = fin[core]
    out_ref[:, theirs] = rest[...]


def scatter_bufs():
    def three(*lead):
        return [pltpu.VMEM(lead + (width,), jnp.bfloat16) for _, width in PIECES]

    return [
        pltpu.VMEM((4, 4, 4, 16, 1024), jnp.bfloat16),
        three(3, 4, 4, 16),
        three(3, 4, 16),
        three(3, 16),
        three(4, 4, 16),
        three(4, 16),
        pltpu.VMEM((2, 8, 1024), jnp.float32),
        pltpu.VMEM((8, 1024), jnp.float32),
    ]


SCALE = 1.0 / math.sqrt(DH)
EXP2_SCALE = SCALE * math.log2(math.e)


def dot(a, b):
    return jnp.dot(a, b, preferred_element_type=jnp.float32)


def dot_nt(a, b):
    return lax.dot_general(a, b, (((1,), (1,)), ((), ())), preferred_element_type=jnp.float32)


def low(a):
    return a.astype(jnp.bfloat16)


def softmax_blocks(query, key_blocks, biases):
    scores = [dot_nt(key, query) for key in key_blocks]
    scores = [s if b is None else s + b for s, b in zip(scores, biases)]
    peak = functools.reduce(
        jnp.maximum, [jnp.max(s, axis=0, keepdims=True) for s in scores]
    )
    raised = [jnp.exp2((s - peak) * EXP2_SCALE) for s in scores]
    inverse = 1.0 / sum(jnp.sum(r, axis=0, keepdims=True) for r in raised)
    return [r * inverse for r in raised]


def score_grads(shares, value_blocks, upstream):
    grads = [dot_nt(value, upstream) for value in value_blocks]
    total = sum(jnp.sum(s * g, axis=0, keepdims=True) for s, g in zip(shares, grads))
    return [low(s * (g - total)) for s, g in zip(shares, grads)]


def row_head(head, qr, kr, vr, ur, attn, attn_t, dq, dk, dv, bias, key_t, value_t, dk_acc, dv_acc):
    lanes = pl.ds(pl.multiple_of(head * DH, DH), DH)
    key_t[...] = kr[:, lanes].T
    value_t[...] = vr[:, lanes].T
    for i in range(4):
        here = pl.ds(i * 256, 256)
        query, upstream = qr[here, lanes], ur[here, lanes]
        spans = [pl.ds(j * 256, 256) for j in range(i + 1)]
        shares = softmax_blocks(
            query, [kr[span, lanes] for span in spans], [None] * i + [bias[0]]
        )
        lows = [low(share) for share in shares]
        out_t = low(sum(dot(value_t[:, span], share) for span, share in zip(spans, lows)))
        attn_t[pl.ds(pl.multiple_of(head * DH, DH), DH), here] = out_t
        attn[here, lanes] = out_t.T
        grads = score_grads(shares, [vr[span, lanes] for span in spans], upstream)
        for j, span in enumerate(spans):
            to_value, to_key = dot(lows[j], upstream), dot(grads[j], query)
            if j == i:
                dv_acc[span] = to_value
                dk_acc[span] = to_key
            else:
                dv_acc[span] += to_value
                dk_acc[span] += to_key
        to_query = sum(dot(key_t[:, span], grad) for span, grad in zip(spans, grads))
        dq[here, lanes] = low(to_query.T * SCALE)
    dk[:, lanes] = low(dk_acc[...] * SCALE)
    dv[:, lanes] = low(dv_acc[...])


def column_block(ref, half, group, lanes):
    return ref[pl.ds(half * 16, 16), pl.ds(group, 16), lanes].reshape(256, DH)


def put_column(ref, half, group, lanes, block):
    ref[pl.ds(half * 16, 16), pl.ds(group, 16), lanes] = low(block).reshape(16, 16, DH)


def column_place(unit):
    group = pl.multiple_of((unit // 4) * 16, 16)
    return group, pl.ds(pl.multiple_of((unit % 4) * DH, DH), DH)


def column_forward(unit, cin, cout, bias, kept):
    group, lanes = column_place(unit)
    key = [column_block(cin[1], half, group, lanes) for half in range(2)]
    value_t = [column_block(cin[2], half, group, lanes).T for half in range(2)]
    slot = 0
    for i in range(2):
        query = column_block(cin[0], i, group, lanes)
        shares = softmax_blocks(query, key[: i + 1], [bias[1]] * i + [bias[2]])
        for share in shares:
            kept[unit, slot] = share
            slot += 1
        out_t = sum(dot(value_t[j], low(share)) for j, share in enumerate(shares))
        put_column(cout[0], i, group, lanes, out_t.T)


def column_backward(unit, cin, cout, kept):
    group, lanes = column_place(unit)
    key = [column_block(cin[1], half, group, lanes) for half in range(2)]
    key_t = [block.T for block in key]
    value = [column_block(cin[2], half, group, lanes) for half in range(2)]
    to_key, to_value = [0.0, 0.0], [0.0, 0.0]
    slot = 0
    for i in range(2):
        query = column_block(cin[0], i, group, lanes)
        upstream = column_block(cin[3], i, group, lanes)
        shares = [kept[unit, slot + j] for j in range(i + 1)]
        slot += i + 1
        grads = score_grads(shares, value[: i + 1], upstream)
        for j in range(i + 1):
            to_value[j] = to_value[j] + dot(low(shares[j]), upstream)
            to_key[j] = to_key[j] + dot(grads[j], query)
        to_query = sum(dot(key_t[j], grad) for j, grad in enumerate(grads))
        put_column(cout[1], i, group, lanes, to_query.T * SCALE)
    for j in range(2):
        put_column(cout[2], j, group, lanes, to_key[j] * SCALE)
        put_column(cout[3], j, group, lanes, to_value[j])


def mega_kernel(factor, *refs):
    q_in, k_in, v_in, w_in, cot_in = refs[:5]
    out_hbm, dq_hbm, dk_hbm, dv_hbm, grad_out = refs[5:10]
    (
        pair,
        full,
        cot,
        rows_in,
        u_row,
        u_col,
        cin,
        cout,
        attn,
        attn_t,
        rows_out,
        accs,
        trans,
        grad,
        layer,
        bias,
        kept,
        bufs,
        ag_send,
        ag_recv,
        rs_send,
        rs_recv,
        go_send,
        go_recv,
        go_local,
        back_send,
        back_recv,
        back_local,
        load,
        store,
    ) = refs[10:]
    s = lax.axis_index("seq")
    p = lax.axis_index("dp")
    row_half, col_half = pl.ds(0, 512), pl.ds(512, 512)
    loads = [pltpu.make_async_copy(cot_in, cot, load.at[0])] + [
        pltpu.make_async_copy(src.at[:, row_half], dst, load.at[1 + t])
        for t, (src, dst) in enumerate(zip((q_in, k_in, v_in), rows_in))
    ]
    for copy in loads:
        copy.start()

    def go_src(t, to):
        if t == 3:
            return u_col.at[pl.ds(to * 32, 32)]
        return (q_in, k_in, v_in)[t].at[pl.ds(to * 32, 32), col_half]

    def go_start(t):
        @pl.loop(1, 32)
        def _(k):
            to = (s + k) % 32
            remote(go_src(t, to), cin[t].at[s], go_send.at[t], go_recv.at[t], (to, p)).start()

        pltpu.make_async_copy(go_src(t, s), cin[t].at[s], go_local.at[t]).start()

    def go_wait(t):
        pltpu.make_async_copy(go_src(t, s), cin[t].at[s], go_local.at[t]).wait()
        wait_bytes(cin[t].at[pl.ds(0, 31)], go_recv.at[t])

    def back_dst(t):
        whole = (attn, dq_hbm, dk_hbm, dv_hbm)[t]
        return whole.at[pl.ds(s * 32, 32), col_half]

    def back_start(t, first=1, end=32):
        @pl.loop(first, end)
        def _(k):
            to = (s + k) % 32
            remote(cout[t].at[to], back_dst(t), back_send.at[t], back_recv.at[t], (to, p)).start()

        if first == 1:
            pltpu.make_async_copy(cout[t].at[s], back_dst(t), back_local.at[t]).start()

    def back_wait(t):
        pltpu.make_async_copy(cout[t].at[s], back_dst(t), back_local.at[t]).wait()
        wait_bytes(cout[t].at[pl.ds(0, 31)], back_recv.at[t])

    greet(True, True)
    gather_start(w_in, pair, full, ag_send, ag_recv, load.at[4])
    gather_send(0, full, ag_send, ag_recv)
    go_start(1)
    lane = lax.broadcasted_iota(jnp.int32, (256, 256), 1)
    sub = lax.broadcasted_iota(jnp.int32, (256, 256), 0)
    same = lane % 16 == sub % 16
    bias[0] = jnp.where(sub <= lane, 0.0, -jnp.inf)
    bias[1] = jnp.where(same, 0.0, -jnp.inf)
    bias[2] = jnp.where(same & (sub <= lane), 0.0, -jnp.inf)
    gather_wait(0, full, ag_recv)
    gather_send(1, full, ag_send, ag_recv)
    go_start(0)
    gather_wait(1, full, ag_recv)
    gather_send(2, full, ag_send, ag_recv)
    go_start(2)
    gather_wait(2, full, ag_recv)
    last = gather_last(full, ag_send, ag_recv)
    last.start()
    last.wait_recv()
    loads[0].wait()

    def upstream_part(y, dst):
        weight = full.at[y]
        place_at = (y % 2) * 256

        @pl.loop(0, 2)
        def _(block):
            here = pl.ds(pl.multiple_of(block * 512, 512), 512)
            dst[here, pl.ds(place_at, 256)] = low(
                dot_nt(cot[here, :], weight[...].reshape(256, 2048))
            )

    upstream_part(2, u_col)
    upstream_part(3, u_col)
    go_start(3)
    upstream_part(0, u_row)
    upstream_part(1, u_row)
    for copy in loads[1:]:
        copy.wait()

    def row_heads(first, end):
        @pl.loop(first, end)
        def _(head):
            row_head(head, *rows_in, u_row, attn, attn_t, *rows_out, bias, *trans, *accs)

    for t in range(3):
        go_wait(t)

    @pl.loop(0, 8)
    def _(unit):
        column_forward(unit, cin, cout, bias, kept)

    back_start(0)
    row_heads(0, 2)
    go_wait(3)

    @pl.loop(0, 8)
    def _(unit):
        column_backward(unit, cin, cout, kept)

    back_start(3)
    row_heads(2, 4)
    row_stores = [
        pltpu.make_async_copy(src, dst.at[:, row_half], store.at[t])
        for t, (src, dst) in enumerate(zip(rows_out, (dq_hbm, dk_hbm, dv_hbm)))
    ]
    for copy in row_stores:
        copy.start()

    def grad_part(half):
        @pl.loop(0, 8)
        def _(block):
            cols = pl.ds(pl.multiple_of(block * 256, 256), 256)
            part = dot(attn_t[pl.ds(half * 512, 512), :], cot[:, cols])
            grad[pl.ds(half * 2, 2), :, :, :, cols] = low(part).reshape(2, 4, 4, 16, 256)

    grad_part(0)
    swap_start(0, grad, bufs[0], rs_send, rs_recv)
    back_wait(0)

    @pl.loop(0, 4)
    def _(block):
        here = pl.ds(pl.multiple_of(block * 256, 256), 256)
        attn_t[pl.ds(512, 512), here] = attn[here, col_half].T

    grad_part(1)
    swap_start(1, grad, bufs[0], rs_send, rs_recv)

    def meanwhile(stage):
        if stage > 0:
            for t, first, end in (((2, 16, 32),), ((1, 1, 32),))[stage - 1]:
                back_start(t, first, end)
            return
        back_start(2, 1, 16)

        @pl.loop(0, 8)
        def _(block):
            cols = pl.ds(pl.multiple_of(block * 256, 256), 256)
            layer[:, cols] = low(dot(attn[...], full[:, :, :, :, cols].reshape(1024, 256)))
            pltpu.make_async_copy(layer.at[:, cols], out_hbm.at[:, cols], store.at[3]).start()

    scatter_grad(grad, grad_out, bufs, rs_send, rs_recv, factor, meanwhile)
    pltpu.make_async_copy(layer, out_hbm, store.at[3]).wait()
    for copy in row_stores:
        copy.wait()
    for stage in range(3):
        gather_wait(stage, full, ag_send)
    last.wait_send()
    for t in (3, 2, 1):
        back_wait(t)
    for t in range(4):
        wait_bytes(cout[t].at[pl.ds(0, 31)], back_send.at[t])
        wait_bytes(cin[t].at[pl.ds(0, 31)], go_send.at[t])


ANY = pl.BlockSpec(memory_space=pl.ANY)
INV = pl.BlockSpec(memory_space=pltpu.VMEM)


def body(queries, keys, values, out_weight, cotangent):
    def vmem(*shape, dtype=jnp.bfloat16):
        return pltpu.VMEM(shape, dtype)

    def dma(count):
        return pltpu.SemaphoreType.DMA((count,))

    half = [1024, 512]
    shapes = [(1024, 2048), (1024, 1024), (1024, 1024), (1024, 1024)]
    results = pl.pallas_call(
        functools.partial(mega_kernel, 1.0 / math.sqrt(4 * 32 * 1024)),
        out_shape=[jax.ShapeDtypeStruct(shape, jnp.bfloat16) for shape in shapes]
        + [jax.ShapeDtypeStruct((8, 2048), jnp.float32)],
        in_specs=[ANY] * 5,
        out_specs=[ANY] * 4 + [INV],
        scratch_shapes=[
            vmem(2, 8, 2048),
            vmem(4, 4, 4, 16, 2048),
            vmem(1024, 2048),
            [vmem(*half) for _ in range(3)],
            vmem(*half),
            vmem(*half),
            [vmem(32, 32, 512) for _ in range(4)],
            [vmem(32, 32, 512) for _ in range(4)],
            vmem(1024, 1024),
            vmem(1024, 1024),
            [vmem(*half) for _ in range(3)],
            [vmem(1024, DH, dtype=jnp.float32) for _ in range(2)],
            [vmem(DH, 1024) for _ in range(2)],
            vmem(4, 4, 4, 16, 2048),
            vmem(1024, 2048),
            vmem(3, 256, 256, dtype=jnp.float32),
            vmem(8, 3, 256, 256, dtype=jnp.float32),
            scatter_bufs(),
            dma(11),
            dma(11),
            dma(11),
            dma(11),
            dma(4),
            dma(4),
            dma(4),
            dma(4),
            dma(4),
            dma(4),
            dma(5),
            dma(4),
        ],
        compiler_params=pltpu.CompilerParams(
            collective_id=1, has_side_effects=True, vmem_limit_bytes=VMEM_LIMIT
        ),
    )(
        *[member.reshape(1024, 1024) for member in (queries, keys, values)],
        out_weight,
        cotangent.reshape(1024, 2048),
    )
    return (
        results[0].reshape(1, 1, 1024, 2048),
        results[1].reshape(1, 1, 1024, 1024),
        results[2].reshape(1, 1, 1024, 1024),
        results[3].reshape(1, 1, 1024, 1024),
        results[4],
    )


def solution(mesh):
    return jax.shard_map(
        body,
        mesh=mesh,
        in_specs=(
            P("dp", "seq", None, None),
            P("dp", "seq", None, None),
            P("dp", "seq", None, None),
            P(("seq", "dp"), None),
            P("dp", "seq", None, None),
        ),
        out_specs=(
            P("dp", "seq", None, None),
            P("dp", "seq", None, None),
            P("dp", "seq", None, None),
            P("dp", "seq", None, None),
            P(("seq", "dp"), None),
        ),
        check_vma=False,
    )
```

```python
import functools
import math

import jax
import jax.numpy as jnp
from jax import lax
from jax.experimental import pallas as pl
from jax.experimental.pallas import tpu as pltpu
from jax.sharding import PartitionSpec as P

ROW_HEADS = 4
COL_HEADS = 4
DH = 128
MESH = pl.DeviceIdType.MESH
VMEM_LIMIT = 67000000
PIECES = ((0, 384), (384, 384), (768, 256))
ORDERS = ((2, 1, 0), (1, 0, 2), (0, 2, 1))


def place():
    s = lax.axis_index("seq")
    p = lax.axis_index("dp")
    return (s // 8, (s // 2) % 4, (s % 2) * 2 + p // 2), p % 2


def device(at, core):
    y, x, z = at
    return ((y * 4 + x) * 2 + z // 2, (z % 2) * 2 + core)


def shifted(at, axis, step):
    moved = list(at)
    moved[axis] = (at[axis] + step) % 4
    return tuple(moved)


def greet(seq_peers, ring_peers):
    s = lax.axis_index("seq")
    p = lax.axis_index("dp")
    at, core = place()
    barrier = pltpu.get_barrier_semaphore()
    count = 0
    if seq_peers:

        @pl.loop(1, 32)
        def _(k):
            pl.semaphore_signal(
                barrier, inc=1, device_id=((s + k) % 32, p), device_id_type=MESH
            )

        count += 31
    if ring_peers:
        pl.semaphore_signal(barrier, inc=1, device_id=device(at, 1 - core), device_id_type=MESH)
        count += 1
        for axis in range(3):
            for step in range(1, 4):
                pl.semaphore_signal(
                    barrier,
                    inc=1,
                    device_id=device(shifted(at, axis, step), core),
                    device_id_type=MESH,
                )
                count += 1
    pl.semaphore_wait(barrier, count)


def remote(src, dst, send, recv, to):
    return pltpu.make_async_remote_copy(
        src_ref=src, dst_ref=dst, send_sem=send, recv_sem=recv, device_id=to, device_id_type=MESH
    )


def wait_bytes(ref, sem):
    pltpu.make_async_copy(ref, ref, sem).wait()


def gather_start(w_ref, pair, full, send, recv, local):
    at, core = place()
    swap = remote(w_ref, pair.at[core], send.at[0], recv.at[0], device(at, 1 - core))
    swap.start()
    own = pltpu.make_async_copy(w_ref, pair.at[core], local)
    own.start()
    own.wait()
    swap.wait()
    half = pl.ds(pl.multiple_of(core * 1024, 128), 1024)
    full[at[0], at[1], at[2], :, half] = jnp.concatenate(
        [pair[0, :, half], pair[1, :, half]], axis=0
    )


def gather_send(stage, full, send, recv):
    at, core = place()
    for k, ((start, width), order) in enumerate(zip(PIECES, ORDERS)):
        index = tuple(pl.ds(0, 4) if axis in order[:stage] else at[axis] for axis in range(3))
        cols = pl.ds(pl.multiple_of(core * 1024 + start, 128), width)
        region = full.at[index + (slice(None), cols)]
        for step in range(1, 4):
            to = device(shifted(at, order[stage], step), core)
            sem = 1 + 3 * stage + k
            remote(region, region, send.at[sem], recv.at[sem], to).start()


def gather_wait(stage, full, sems):
    at, core = place()
    for k, ((start, width), order) in enumerate(zip(PIECES, ORDERS)):
        index = tuple(
            pl.ds(0, 3)
            if axis == order[stage]
            else (pl.ds(0, 4) if axis in order[:stage] else at[axis])
            for axis in range(3)
        )
        wait_bytes(full.at[index + (slice(None), pl.ds(0, width))], sems.at[1 + 3 * stage + k])


def gather_last(full, send, recv):
    at, core = place()
    mine = full.at[:, :, :, :, pl.ds(pl.multiple_of(core * 1024, 128), 1024)]
    return remote(mine, mine, send.at[10], recv.at[10], device(at, 1 - core))


def swap_start(half, g_ref, chip, send, recv):
    at, core = place()
    rows = pl.ds(half * 2, 2)
    theirs = pl.ds(pl.multiple_of((1 - core) * 1024, 128), 1024)
    src = g_ref.at[rows, :, :, :, theirs]
    remote(src, chip.at[rows], send.at[0], recv.at[0], device(at, 1 - core)).start()


def scatter_grad(g_ref, out_ref, bufs, send, recv, factor, meanwhile):
    chip, firsts, seconds, thirds, sums1, sums2, fin, rest = bufs
    at, core = place()
    other = device(at, 1 - core)
    mine = pl.ds(pl.multiple_of(core * 1024, 128), 1024)
    theirs = pl.ds(pl.multiple_of((1 - core) * 1024, 128), 1024)
    wait_bytes(chip, recv.at[0])

    @pl.loop(0, 4)
    def _(y):
        @pl.loop(0, 4)
        def _(x):
            total = chip[y, x].astype(jnp.float32) + g_ref[y, x, :, :, mine].astype(jnp.float32)
            chip[y, x] = total.astype(jnp.bfloat16)

    sem = 1
    for stage in range(3):
        for k, ((start, width), order) in enumerate(zip(PIECES, ORDERS)):
            path = order[::-1]
            axis = path[stage]
            left = [a for a in range(3) if a not in path[:stage]]
            for step in range(1, 4):
                to = shifted(at, axis, step)
                index = tuple(to[a] if a == axis else slice(None) for a in left)
                if stage == 0:
                    src = chip.at[index + (slice(None), pl.ds(start, width))]
                    dst = firsts[k].at[step - 1]
                elif stage == 1:
                    src = sums1[k].at[index]
                    dst = seconds[k].at[step - 1]
                else:
                    src = sums2[k].at[index]
                    dst = thirds[k].at[step - 1]
                remote(src, dst, send.at[sem], recv.at[sem], device(to, core)).start()
            sem += 1
        meanwhile(stage)
        for k, ((start, width), order) in enumerate(zip(PIECES, ORDERS)):
            path = order[::-1]
            axis = path[stage]
            left = [a for a in range(3) if a not in path[:stage]]
            index = tuple(at[a] if a == axis else slice(None) for a in left)
            got = (firsts, seconds, thirds)[stage][k]
            wait_bytes(got, recv.at[sem - 3 + k])
            wait_bytes(got, send.at[sem - 3 + k])
            if stage == 0:
                own = chip[index + (slice(None), pl.ds(start, width))]
            elif stage == 1:
                own = sums1[k][index]
            else:
                own = sums2[k][index]
            total = own.astype(jnp.float32)
            for step in range(3):
                total = total + got[step].astype(jnp.float32)
            if stage == 0:
                sums1[k][...] = total.astype(jnp.bfloat16)
            elif stage == 1:
                sums2[k][...] = total.astype(jnp.bfloat16)
            else:
                for low in range(2):
                    fin[low, :, pl.ds(start, width)] = total[low * 8 : low * 8 + 8] * factor
    last = remote(fin.at[1 - core], rest, send.at[sem], recv.at[sem], other)
    last.start()
    last.wait()
    wait_bytes(chip, send.at[0])
    out_ref[:, mine] = fin[core]
    out_ref[:, theirs] = rest[...]


def scatter_bufs():
    def three(*lead):
        return [pltpu.VMEM(lead + (width,), jnp.bfloat16) for _, width in PIECES]

    return [
        pltpu.VMEM((4, 4, 4, 16, 1024), jnp.bfloat16),
        three(3, 4, 4, 16),
        three(3, 4, 16),
        three(3, 16),
        three(4, 4, 16),
        three(4, 16),
        pltpu.VMEM((2, 8, 1024), jnp.float32),
        pltpu.VMEM((8, 1024), jnp.float32),
    ]


SCALE = 1.0 / math.sqrt(DH)
EXP2_SCALE = SCALE * math.log2(math.e)


def dot(a, b):
    return jnp.dot(a, b, preferred_element_type=jnp.float32)


def dot_nt(a, b):
    return lax.dot_general(a, b, (((1,), (1,)), ((), ())), preferred_element_type=jnp.float32)


def low(a):
    return a.astype(jnp.bfloat16)


def softmax_blocks(query, key_blocks, biases):
    scores = [dot_nt(key, query) for key in key_blocks]
    scores = [s if b is None else s + b for s, b in zip(scores, biases)]
    peak = functools.reduce(
        jnp.maximum, [jnp.max(s, axis=0, keepdims=True) for s in scores]
    )
    raised = [jnp.exp2((s - peak) * EXP2_SCALE) for s in scores]
    inverse = 1.0 / sum(jnp.sum(r, axis=0, keepdims=True) for r in raised)
    return [r * inverse for r in raised]


def score_grads(shares, value_blocks, upstream):
    grads = [dot_nt(value, upstream) for value in value_blocks]
    total = sum(jnp.sum(s * g, axis=0, keepdims=True) for s, g in zip(shares, grads))
    return [low(s * (g - total)) for s, g in zip(shares, grads)]


def row_head(head, qr, kr, vr, ur, attn, attn_t, dq, dk, dv, bias, key_t, value_t, dk_acc, dv_acc):
    lanes = pl.ds(pl.multiple_of(head * DH, DH), DH)
    key_t[...] = kr[:, lanes].T
    value_t[...] = vr[:, lanes].T
    for i in range(4):
        here = pl.ds(i * 256, 256)
        query, upstream = qr[here, lanes], ur[here, lanes]
        spans = [pl.ds(j * 256, 256) for j in range(i + 1)]
        shares = softmax_blocks(
            query, [kr[span, lanes] for span in spans], [None] * i + [bias[0]]
        )
        lows = [low(share) for share in shares]
        out_t = low(sum(dot(value_t[:, span], share) for span, share in zip(spans, lows)))
        attn_t[pl.ds(pl.multiple_of(head * DH, DH), DH), here] = out_t
        attn[here, lanes] = out_t.T
        grads = score_grads(shares, [vr[span, lanes] for span in spans], upstream)
        for j, span in enumerate(spans):
            to_value, to_key = dot(lows[j], upstream), dot(grads[j], query)
            if j == i:
                dv_acc[span] = to_value
                dk_acc[span] = to_key
            else:
                dv_acc[span] += to_value
                dk_acc[span] += to_key
        to_query = sum(dot(key_t[:, span], grad) for span, grad in zip(spans, grads))
        dq[here, lanes] = low(to_query.T * SCALE)
    dk[:, lanes] = low(dk_acc[...] * SCALE)
    dv[:, lanes] = low(dv_acc[...])


def column_block(ref, half, group, lanes):
    return ref[pl.ds(half * 16, 16), pl.ds(group, 16), lanes].reshape(256, DH)


def put_column(ref, half, group, lanes, block):
    ref[pl.ds(half * 16, 16), pl.ds(group, 16), lanes] = low(block).reshape(16, 16, DH)


def column_place(unit):
    group = pl.multiple_of((unit // 4) * 16, 16)
    return group, pl.ds(pl.multiple_of((unit % 4) * DH, DH), DH)


def column_forward(unit, cin, cout, bias, kept):
    group, lanes = column_place(unit)
    key = [column_block(cin[1], half, group, lanes) for half in range(2)]
    value_t = [column_block(cin[2], half, group, lanes).T for half in range(2)]
    slot = 0
    for i in range(2):
        query = column_block(cin[0], i, group, lanes)
        shares = softmax_blocks(query, key[: i + 1], [bias[1]] * i + [bias[2]])
        for share in shares:
            kept[unit, slot] = share
            slot += 1
        out_t = sum(dot(value_t[j], low(share)) for j, share in enumerate(shares))
        put_column(cout[0], i, group, lanes, out_t.T)


def column_backward(unit, cin, cout, kept):
    group, lanes = column_place(unit)
    key = [column_block(cin[1], half, group, lanes) for half in range(2)]
    key_t = [block.T for block in key]
    value = [column_block(cin[2], half, group, lanes) for half in range(2)]
    to_key, to_value = [0.0, 0.0], [0.0, 0.0]
    slot = 0
    for i in range(2):
        query = column_block(cin[0], i, group, lanes)
        upstream = column_block(cin[3], i, group, lanes)
        shares = [kept[unit, slot + j] for j in range(i + 1)]
        slot += i + 1
        grads = score_grads(shares, value[: i + 1], upstream)
        for j in range(i + 1):
            to_value[j] = to_value[j] + dot(low(shares[j]), upstream)
            to_key[j] = to_key[j] + dot(grads[j], query)
        to_query = sum(dot(key_t[j], grad) for j, grad in enumerate(grads))
        put_column(cout[1], i, group, lanes, to_query.T * SCALE)
    for j in range(2):
        put_column(cout[2], j, group, lanes, to_key[j] * SCALE)
        put_column(cout[3], j, group, lanes, to_value[j])


def mega_kernel(factor, *refs):
    q_in, k_in, v_in, w_in, cot_in = refs[:5]
    out_hbm, dq_hbm, dk_hbm, dv_hbm, grad_out = refs[5:10]
    (
        pair,
        full,
        cot,
        rows_in,
        u_row,
        u_col,
        cin,
        cout,
        attn,
        attn_t,
        rows_out,
        accs,
        trans,
        grad,
        layer,
        bias,
        kept,
        bufs,
        ag_send,
        ag_recv,
        rs_send,
        rs_recv,
        go_send,
        go_recv,
        go_local,
        back_send,
        back_recv,
        back_local,
        load,
        store,
    ) = refs[10:]
    s = lax.axis_index("seq")
    p = lax.axis_index("dp")
    row_half, col_half = pl.ds(0, 512), pl.ds(512, 512)
    loads = [pltpu.make_async_copy(cot_in, cot, load.at[0])] + [
        pltpu.make_async_copy(src.at[:, row_half], dst, load.at[1 + t])
        for t, (src, dst) in enumerate(zip((q_in, k_in, v_in), rows_in))
    ]
    for copy in loads:
        copy.start()

    def go_src(t, to):
        if t == 3:
            return u_col.at[pl.ds(to * 32, 32)]
        return (q_in, k_in, v_in)[t].at[pl.ds(to * 32, 32), col_half]

    def go_start(t):
        @pl.loop(1, 32)
        def _(k):
            to = (s + k) % 32
            remote(go_src(t, to), cin[t].at[s], go_send.at[t], go_recv.at[t], (to, p)).start()

        pltpu.make_async_copy(go_src(t, s), cin[t].at[s], go_local.at[t]).start()

    def go_wait(t):
        pltpu.make_async_copy(go_src(t, s), cin[t].at[s], go_local.at[t]).wait()
        wait_bytes(cin[t].at[pl.ds(0, 31)], go_recv.at[t])

    def back_dst(t):
        whole = (attn, dq_hbm, dk_hbm, dv_hbm)[t]
        return whole.at[pl.ds(s * 32, 32), col_half]

    def back_start(t, first=1, end=32):
        @pl.loop(first, end)
        def _(k):
            to = (s + k) % 32
            remote(cout[t].at[to], back_dst(t), back_send.at[t], back_recv.at[t], (to, p)).start()

        if first == 1:
            pltpu.make_async_copy(cout[t].at[s], back_dst(t), back_local.at[t]).start()

    def back_wait(t):
        pltpu.make_async_copy(cout[t].at[s], back_dst(t), back_local.at[t]).wait()
        wait_bytes(cout[t].at[pl.ds(0, 31)], back_recv.at[t])

    greet(True, True)
    gather_start(w_in, pair, full, ag_send, ag_recv, load.at[4])
    gather_send(0, full, ag_send, ag_recv)
    go_start(1)
    lane = lax.broadcasted_iota(jnp.int32, (256, 256), 1)
    sub = lax.broadcasted_iota(jnp.int32, (256, 256), 0)
    same = lane % 16 == sub % 16
    bias[0] = jnp.where(sub <= lane, 0.0, -jnp.inf)
    bias[1] = jnp.where(same, 0.0, -jnp.inf)
    bias[2] = jnp.where(same & (sub <= lane), 0.0, -jnp.inf)
    gather_wait(0, full, ag_recv)
    gather_send(1, full, ag_send, ag_recv)
    go_start(0)
    gather_wait(1, full, ag_recv)
    gather_send(2, full, ag_send, ag_recv)
    go_start(2)
    gather_wait(2, full, ag_recv)
    last = gather_last(full, ag_send, ag_recv)
    last.start()
    last.wait_recv()
    loads[0].wait()

    def upstream_part(y, dst):
        weight = full.at[y]
        place_at = (y % 2) * 256

        @pl.loop(0, 2)
        def _(block):
            here = pl.ds(pl.multiple_of(block * 512, 512), 512)
            dst[here, pl.ds(place_at, 256)] = low(
                dot_nt(cot[here, :], weight[...].reshape(256, 2048))
            )

    upstream_part(2, u_col)
    upstream_part(3, u_col)
    go_start(3)
    upstream_part(0, u_row)
    upstream_part(1, u_row)
    for copy in loads[1:]:
        copy.wait()

    def row_heads(first, end):
        @pl.loop(first, end)
        def _(head):
            row_head(head, *rows_in, u_row, attn, attn_t, *rows_out, bias, *trans, *accs)

    for t in range(3):
        go_wait(t)

    @pl.loop(0, 8)
    def _(unit):
        column_forward(unit, cin, cout, bias, kept)

    back_start(0)
    row_heads(0, 2)
    go_wait(3)

    @pl.loop(0, 8)
    def _(unit):
        column_backward(unit, cin, cout, kept)

    back_start(3)
    row_heads(2, 4)
    row_stores = [
        pltpu.make_async_copy(src, dst.at[:, row_half], store.at[t])
        for t, (src, dst) in enumerate(zip(rows_out, (dq_hbm, dk_hbm, dv_hbm)))
    ]
    for copy in row_stores:
        copy.start()

    def grad_part(half):
        @pl.loop(0, 8)
        def _(block):
            cols = pl.ds(pl.multiple_of(block * 256, 256), 256)
            part = dot(attn_t[pl.ds(half * 512, 512), :], cot[:, cols])
            grad[pl.ds(half * 2, 2), :, :, :, cols] = low(part).reshape(2, 4, 4, 16, 256)

    grad_part(0)
    swap_start(0, grad, bufs[0], rs_send, rs_recv)
    back_wait(0)

    @pl.loop(0, 4)
    def _(block):
        here = pl.ds(pl.multiple_of(block * 256, 256), 256)
        attn_t[pl.ds(512, 512), here] = attn[here, col_half].T

    grad_part(1)
    swap_start(1, grad, bufs[0], rs_send, rs_recv)

    def meanwhile(stage):
        if stage > 0:
            for t, first, end in (((2, 16, 32),), ((1, 1, 32),))[stage - 1]:
                back_start(t, first, end)
            return
        back_start(2, 1, 16)

        @pl.loop(0, 8)
        def _(block):
            cols = pl.ds(pl.multiple_of(block * 256, 256), 256)
            layer[:, cols] = low(dot(attn[...], full[:, :, :, :, cols].reshape(1024, 256)))
            pltpu.make_async_copy(layer.at[:, cols], out_hbm.at[:, cols], store.at[3]).start()

    scatter_grad(grad, grad_out, bufs, rs_send, rs_recv, factor, meanwhile)
    pltpu.make_async_copy(layer, out_hbm, store.at[3]).wait()
    for copy in row_stores:
        copy.wait()
    for stage in range(3):
        gather_wait(stage, full, ag_send)
    last.wait_send()
    for t in (3, 2, 1):
        back_wait(t)
    for t in range(4):
        wait_bytes(cout[t].at[pl.ds(0, 31)], back_send.at[t])
        wait_bytes(cin[t].at[pl.ds(0, 31)], go_send.at[t])


ANY = pl.BlockSpec(memory_space=pl.ANY)
INV = pl.BlockSpec(memory_space=pltpu.VMEM)


def settle_kernel(*refs):
    srcs, dsts, held = refs[:5], refs[5:10], refs[10:15]
    came, left = refs[15:]
    chunks = []
    for t, src in enumerate(srcs):
        count = src.shape[0]
        step = min(count, 256)
        for start in range(0, count, step):
            chunks.append((t, pl.ds(start, step)))
    ins = [
        pltpu.make_async_copy(srcs[t].at[rows], held[t].at[rows], came.at[n])
        for n, (t, rows) in enumerate(chunks)
    ]
    outs = [
        pltpu.make_async_copy(held[t].at[rows], dsts[t].at[rows], left.at[n])
        for n, (t, rows) in enumerate(chunks)
    ]
    for copy in ins:
        copy.start()
    for coming, going in zip(ins, outs):
        coming.wait()
        going.start()
    for copy in outs:
        copy.wait()


def settle(arrays):
    shapes = [jax.ShapeDtypeStruct(member.shape, member.dtype) for member in arrays]
    return pl.pallas_call(
        settle_kernel,
        out_shape=shapes,
        in_specs=[ANY] * 5,
        out_specs=[ANY] * 5,
        scratch_shapes=[pltpu.VMEM(shape.shape, shape.dtype) for shape in shapes]
        + [pltpu.SemaphoreType.DMA((17,))] * 2,
        compiler_params=pltpu.CompilerParams(vmem_limit_bytes=VMEM_LIMIT),
    )(*arrays)


def body(queries, keys, values, out_weight, cotangent):
    def vmem(*shape, dtype=jnp.bfloat16):
        return pltpu.VMEM(shape, dtype)

    def dma(count):
        return pltpu.SemaphoreType.DMA((count,))

    half = [1024, 512]
    shapes = [(1024, 2048), (1024, 1024), (1024, 1024), (1024, 1024)]
    results = pl.pallas_call(
        functools.partial(mega_kernel, 1.0 / math.sqrt(4 * 32 * 1024)),
        out_shape=[jax.ShapeDtypeStruct(shape, jnp.bfloat16) for shape in shapes]
        + [jax.ShapeDtypeStruct((8, 2048), jnp.float32)],
        in_specs=[ANY] * 5,
        out_specs=[ANY] * 4 + [INV],
        scratch_shapes=[
            vmem(2, 8, 2048),
            vmem(4, 4, 4, 16, 2048),
            vmem(1024, 2048),
            [vmem(*half) for _ in range(3)],
            vmem(*half),
            vmem(*half),
            [vmem(32, 32, 512) for _ in range(4)],
            [vmem(32, 32, 512) for _ in range(4)],
            vmem(1024, 1024),
            vmem(1024, 1024),
            [vmem(*half) for _ in range(3)],
            [vmem(1024, DH, dtype=jnp.float32) for _ in range(2)],
            [vmem(DH, 1024) for _ in range(2)],
            vmem(4, 4, 4, 16, 2048),
            vmem(1024, 2048),
            vmem(3, 256, 256, dtype=jnp.float32),
            vmem(8, 3, 256, 256, dtype=jnp.float32),
            scatter_bufs(),
            dma(11),
            dma(11),
            dma(11),
            dma(11),
            dma(4),
            dma(4),
            dma(4),
            dma(4),
            dma(4),
            dma(4),
            dma(5),
            dma(4),
        ],
        compiler_params=pltpu.CompilerParams(
            collective_id=1, has_side_effects=True, vmem_limit_bytes=VMEM_LIMIT
        ),
    )(
        *[member.reshape(1024, 1024) for member in (queries, keys, values)],
        out_weight,
        cotangent.reshape(1024, 2048),
    )
    results = settle(results)
    return (
        results[0].reshape(1, 1, 1024, 2048),
        results[1].reshape(1, 1, 1024, 1024),
        results[2].reshape(1, 1, 1024, 1024),
        results[3].reshape(1, 1, 1024, 1024),
        results[4],
    )


def solution(mesh):
    return jax.shard_map(
        body,
        mesh=mesh,
        in_specs=(
            P("dp", "seq", None, None),
            P("dp", "seq", None, None),
            P("dp", "seq", None, None),
            P(("seq", "dp"), None),
            P("dp", "seq", None, None),
        ),
        out_specs=(
            P("dp", "seq", None, None),
            P("dp", "seq", None, None),
            P("dp", "seq", None, None),
            P("dp", "seq", None, None),
            P(("seq", "dp"), None),
        ),
        check_vma=False,
    )
```
